32 devices in a mesh: tok: 8 (over z, y), wa: 2 (over x), wb: 2 (over core).
Axes of the slice: x: 2, y: 2, z: 4, core: 2. Of those that a mesh axis runs over, the one named last changes fastest.
Arguments:
- tokens: bfloat16 [4096, 1024], P(('tok', 'wa', 'wb')), may hold values from -6 to 6
- deal: int32 [4096], P(('tok', 'wa', 'wb')), may hold values from 0 to 4095, as said below
- lengths: int32 [8, 8], P('tok'), may hold values from 1 to 192, 512 in all within a row
- group_ids: int32 [8, 8], P('tok'), may hold values from 0 to 1
- page_table: int32 [2, 4], replicated, may hold values from 0 to 15, as said below
- prefix_cache: bfloat16 [16, 128, 2, 1024], P('tok', None, None, ('wa', 'wb')), may hold values from -12 to 12
- qkv_weight: bfloat16 [1024, 3, 1024], P(None, None, ('wa', 'wb')), may hold values from -0.1875 to 0.1875
- qkv_bias: float32 [3, 1024], P(None, ('wa', 'wb')), may hold values from -9 to 9
- out_weight: bfloat16 [1024, 1024], P(('wa', 'wb')), may hold values from -9 to 9
- out_bias: float32 [1024], replicated, may hold values from -3 to 3
- norm1_gain: float32 [1024], replicated, may hold values from 0.5 to 1.5
- norm1_bias: float32 [1024], replicated, may hold values from -3 to 3
- up_weight: bfloat16 [1024, 4096], P(None, ('wa', 'wb')), may hold values from -0.1875 to 0.1875
- up_bias: float32 [4096], P(('wa', 'wb')), may hold values from -3 to 3
- down_weight: bfloat16 [4096, 1024], P(('wa', 'wb')), may hold values from -0.09375 to 0.09375
- down_bias: float32 [1024], replicated, may hold values from -3 to 3
- norm2_gain: float32 [1024], replicated, may hold values from 0.5 to 1.5
- norm2_bias: float32 [1024], replicated, may hold values from -3 to 3
Outputs:
- hidden: bfloat16 [4096, 1024], P(('tok', 'wa', 'wb'))
- suffix_cache: bfloat16 [4096, 2, 1024], P('tok', None, ('wa', 'wb'))
The draws below stay inside these ranges and needn't reach their ends.
Inputs may be any that keep to these rules, and one draw needn't show every extreme that they name: deal is a permutation of 0 to 4095. For the device at index r of tok and index c of the joined wa+wb axis, its 128 entries are, in some order, (s * 4 + c) * 128 + r * 16 + k over all s < 8 and k < 16. Every row of lengths sums to 512. `page_table`: all entries are distinct slots; slots 0 and 15 are always used. Slot s is held by index s // 2 of tok; one index holds 2 live slots.
All inputs are finite; a program needn't handle non-finite values.
Results may differ from the reference program's by a relative error of at most 0.015.
Values may be sent and summed in bfloat16 or wider, within the bound.
A program may use at most 128 MiB of HBM per device.

```python
import math
import jax
import jax.numpy as jnp
import numpy as np
from jax import lax

D = 1024
HEADS = 16
HEAD = 64
FF = 4096
PAGE = 128
GROUPS = 2
SEQ_DEV = 8
ROW_DEV = 128
BLOCK_DEVS = 4
TOK_DEV = 512
TOKENS = 4096
RUN = 16
SLOTS = 2
POOL = 16
PAGES_G = 4
MOST_LEN = 192
N_TOK = 8


def shuffle_rows(subkey):
    return jax.random.permutation(subkey, ROW_DEV)


def draw_deal(key, part):
    devices_all = TOKENS // ROW_DEV
    subkeys = jax.random.split(key, devices_all)
    orders = jax.vmap(shuffle_rows)(subkeys).astype(jnp.int32)
    device = jnp.arange(devices_all, dtype=jnp.int32)
    row_block = device // BLOCK_DEVS
    column = device % BLOCK_DEVS
    source = orders // RUN
    within = orders % RUN
    value = (source * BLOCK_DEVS + column[:, None]) * ROW_DEV + row_block[:, None] * RUN + within
    return value.reshape(TOKENS).astype(jnp.int32)


def draw_page_table(key, part):
    first, second, third = jax.random.split(key, 3)
    holders = POOL // SLOTS
    full_holder = jax.random.randint(first, (), 0, holders).astype(jnp.int32)
    shuffled = jax.random.permutation(second, POOL).astype(jnp.int32)
    slot_ids = jnp.arange(POOL, dtype=jnp.int32)
    holder = slot_ids // SLOTS
    scores = jnp.where(holder == full_holder, shuffled - POOL, shuffled)
    ends_slot = (slot_ids == 0) | (slot_ids == POOL - 1)
    scores = jnp.where(ends_slot, shuffled - 2 * POOL, scores).astype(jnp.int32)
    picked = jnp.argsort(scores, stable=True)[:GROUPS * PAGES_G].astype(jnp.int32)
    placed = jax.random.permutation(third, picked)
    return placed.reshape(GROUPS, PAGES_G).astype(jnp.int32)


def draw_qkv_bias(key, part):
    noise_key = jax.random.fold_in(key, 523)
    values = jnp.clip(0.3 * jax.random.normal(noise_key, (3, D), jnp.float32), -3.0, 3.0)
    return values.astype(jnp.float32)


def draw_prefix_cache(key, part):
    first = jax.random.fold_in(jax.random.fold_in(key, 277), 0)
    shape = (POOL, PAGE, 2, D)
    values = jnp.clip(jax.random.normal(first, shape, jnp.float32), -6.0, 6.0)
    return values.astype(jnp.bfloat16)


def with_ends(result, stream_key, smallest, top_value):
    longest = result.shape.index(max(result.shape))
    spots = []
    for shift in (0, 1):
        where = [jax.random.randint(jax.random.fold_in(stream_key, axis), (), 0, length) for axis, length in enumerate(result.shape)]
        where[longest] = (where[longest] + shift) % result.shape[longest]
        spots.append(tuple(where))
    return result.at[spots[0]].set(smallest).at[spots[1]].set(top_value)


def level_of(key, shape, cuts, low, largest):
    factor_of = 1.0
    for position, blocks in cuts:
        draws = jax.random.uniform(jax.random.fold_in(jax.random.fold_in(key, 6), position), (blocks,), jnp.float32, low / len(cuts), largest / len(cuts))
        factor_of = factor_of * jnp.repeat(jnp.exp(draws), shape[position] // blocks).reshape((-1,) + (1,) * (len(shape) - 1 - position))
    return factor_of


def profile(count, total, reach, lean):
    loads = [(1 << 20) // math.isqrt(rank ** lean) + 1 for rank in range(2, count + 1)]
    rest, given = total - reach - (count - 1), [1] * (count - 1)
    while rest > 0:
        movable = [i for i in range(count - 1) if given[i] < reach]
        whole, budget = sum([loads[i] for i in movable]), rest
        for i in movable:
            more = min(reach - given[i], max(1, budget * loads[i] // whole), rest)
            given[i] = given[i] + more
            rest = rest - more
    return np.array([reach] + given)


def uneven(rng, number_of, total, reach, lean):
    if number_of == 2:
        one = jax.random.randint(rng, (), max(1, total - reach), min(reach, total - 1) + 1)
        return jnp.stack([one, total - one])
    sizes = jnp.asarray(profile(number_of, total, reach, lean), jnp.int32)
    couples = (number_of - 1) // 2
    giver, sink = sizes[1:1 + 2 * couples:2], sizes[2:2 + 2 * couples:2]
    room = jnp.minimum(giver - 1, reach - sink)
    moved = jax.random.randint(jax.random.fold_in(rng, 1), (couples,), 0, 1 << 20) % (room + 1)
    sizes = sizes.at[1:1 + 2 * couples:2].set(giver - moved).at[2:2 + 2 * couples:2].set(sink + moved)
    return sizes[jax.random.permutation(jax.random.fold_in(rng, 2), number_of)]


def gaussian(stream_key, extent, scale, limit, shards=(), kind=jnp.bfloat16):
    array = scale * jax.random.normal(stream_key, extent, jnp.float32)
    if shards:
        array = array * level_of(stream_key, extent, shards, -0.22, 0.18)
    return jnp.clip(array, -limit, limit).astype(kind)


def setup_inputs(seed: int = 0) -> dict:
    seeds = jax.random.split(jax.random.key(seed), 19)
    return {
        "tokens": gaussian(seeds[0], (TOKENS, D), 1.0, 6.0, ((0, 32),)),
        "deal": draw_deal(jax.random.fold_in(seeds[18], 71), 0),
        "lengths": jax.vmap(lambda own: uneven(own, SEQ_DEV, TOK_DEV, MOST_LEN, 2))(jax.random.split(seeds[2], N_TOK)).reshape((N_TOK, SEQ_DEV)).astype(jnp.int32),
        "group_ids": with_ends(jax.random.randint(seeds[3], (N_TOK, SEQ_DEV), 0, GROUPS), jax.random.fold_in(seeds[3], 1), 0, GROUPS - 1).astype(jnp.int32),
        "page_table": draw_page_table(jax.random.fold_in(seeds[18], 71), 0),
        "prefix_cache": draw_prefix_cache(jax.random.fold_in(seeds[18], 71), 0),
        "qkv_weight": gaussian(seeds[6], (D, 3, D), D ** -0.5, 0.1875, ((2, 4),)),
        "qkv_bias": draw_qkv_bias(jax.random.fold_in(seeds[18], 71), 0),
        "out_weight": gaussian(seeds[8], (D, D), 1.5, 9.0, ((0, 4),)),
        "out_bias": gaussian(seeds[9], (D,), 0.3, 3.0, (), jnp.float32),
        "norm1_gain": jnp.clip(1.0 + 0.1 * jax.random.normal(seeds[10], (D,), jnp.float32), 0.5, 1.5),
        "norm1_bias": gaussian(seeds[11], (D,), 0.3, 3.0, (), jnp.float32),
        "up_weight": gaussian(seeds[12], (D, FF), D ** -0.5, 0.1875, ((1, 4),)),
        "up_bias": gaussian(seeds[13], (FF,), 0.3, 3.0, ((0, 4),), jnp.float32),
        "down_weight": gaussian(seeds[14], (FF, D), FF ** -0.5, 0.09375, ((0, 4),)),
        "down_bias": gaussian(seeds[15], (D,), 0.3, 3.0, (), jnp.float32),
        "norm2_gain": jnp.clip(1.0 + 0.1 * jax.random.normal(seeds[16], (D,), jnp.float32), 0.5, 1.5),
        "norm2_bias": gaussian(seeds[17], (D,), 0.3, 3.0, (), jnp.float32),
    }


def layer_norm(values, gain, bias):
    mean = lax.optimization_barrier(jnp.mean(values, axis=-1, keepdims=True))
    centered = values - mean
    spread = lax.optimization_barrier(jnp.mean(centered * centered, axis=-1, keepdims=True))
    return centered * lax.rsqrt(spread + 1e-05) * gain + bias

def reference(tokens, deal, lengths, group_ids, page_table, prefix_cache, qkv_weight, qkv_bias, out_weight, out_bias, norm1_gain, norm1_bias, up_weight, up_bias, down_weight, down_bias, norm2_gain, norm2_bias):
    scale = 1.0 / math.sqrt(HEAD)
    ordered = jnp.take(tokens, deal, axis=0)
    qkv = jnp.dot(ordered, qkv_weight.reshape(D, 3 * D), preferred_element_type=jnp.float32) + qkv_bias.reshape(3 * D)
    qkv = qkv.astype(jnp.bfloat16).reshape(TOKENS, 3, D)
    suffix_cache = qkv[:, 1:3, :]
    ends = jnp.cumsum(lengths, axis=1).astype(jnp.int32)
    places = jnp.arange(TOK_DEV, dtype=jnp.int32)
    seq = lax.optimization_barrier(jnp.sum((places[None, :, None] >= ends[:, None, :]).astype(jnp.int32), axis=2)).astype(jnp.int32)
    seq_ids = jnp.arange(SEQ_DEV, dtype=jnp.int32)
    row_group = lax.optimization_barrier(jnp.sum(jnp.where(seq[:, :, None] == seq_ids[None, None, :], group_ids[:, None, :], 0), axis=2)).astype(jnp.int32)
    chosen = jnp.take(prefix_cache, page_table.reshape(-1).astype(jnp.int32), axis=0)
    keys_total = GROUPS * PAGES_G * PAGE
    chosen = chosen.reshape(keys_total, 2, HEADS, HEAD)
    prefix_keys = jnp.transpose(chosen[:, 0], (1, 0, 2))
    prefix_values = jnp.transpose(chosen[:, 1], (1, 0, 2))
    key_group = (jnp.arange(keys_total, dtype=jnp.int32) // (PAGES_G * PAGE)).astype(jnp.int32)
    blocks = qkv.reshape(N_TOK, TOK_DEV, 3, HEADS, HEAD)

    def attend_block(inputs):
        block, block_seq, block_group = inputs
        allowed = (block_seq[:, None] == block_seq[None, :]) & (places[None, :] <= places[:, None])
        visible = key_group[None, :] == block_group[:, None]
        queries = jnp.transpose(block[:, 0], (1, 0, 2))
        keys = jnp.transpose(block[:, 1], (1, 0, 2))
        values = jnp.transpose(block[:, 2], (1, 0, 2))

        def attend_head(head_inputs):
            query, key, value, prefix_key, prefix_value = head_inputs
            near = jnp.dot(query, key.T, preferred_element_type=jnp.float32) * scale
            near = jnp.where(allowed, near, -jnp.inf)
            far = jnp.dot(query, prefix_key.T, preferred_element_type=jnp.float32) * scale
            far = jnp.where(visible, far, -jnp.inf)
            top = jnp.maximum(lax.optimization_barrier(jnp.max(near, axis=1)), lax.optimization_barrier(jnp.max(far, axis=1)))
            near_weight = jnp.exp(near - top[:, None])
            far_weight = jnp.exp(far - top[:, None])
            total = lax.optimization_barrier(jnp.sum(near_weight, axis=1)) + lax.optimization_barrier(jnp.sum(far_weight, axis=1))
            summed = jnp.dot(near_weight.astype(jnp.bfloat16), value, preferred_element_type=jnp.float32)
            summed = summed + jnp.dot(far_weight.astype(jnp.bfloat16), prefix_value, preferred_element_type=jnp.float32)
            return summed / total[:, None]
        heads_out = lax.map(attend_head, (queries, keys, values, prefix_keys, prefix_values))
        return jnp.transpose(heads_out, (1, 0, 2)).reshape(TOK_DEV, D)
    attention = lax.map(attend_block, (blocks, seq, row_group)).reshape(TOKENS, D).astype(jnp.bfloat16)
    mixed = jnp.dot(attention, out_weight, preferred_element_type=jnp.float32) + out_bias + ordered.astype(jnp.float32)
    normed = layer_norm(mixed, norm1_gain, norm1_bias).astype(jnp.bfloat16)
    inner = jax.nn.gelu(jnp.dot(normed, up_weight, preferred_element_type=jnp.float32) + up_bias, approximate=False).astype(jnp.bfloat16)
    outer = jnp.dot(inner, down_weight, preferred_element_type=jnp.float32) + down_bias + normed.astype(jnp.float32)
    hidden = layer_norm(outer, norm2_gain, norm2_bias).astype(jnp.bfloat16)
    return (hidden, suffix_cache)
```

```python
import functools
import math

import jax
import jax.numpy as jnp
from jax import lax
from jax.experimental import pallas as pl
from jax.experimental.pallas import tpu as pltpu
from jax.sharding import PartitionSpec as P

HEAD = 64
SEQ_DEV = 8
MOST_LEN = 192
FAR = 3e38
MESH = pl.DeviceIdType.MESH


def layer_norm(values, gain, bias):
    mean = jnp.mean(values, axis=-1, keepdims=True)
    centered = values - mean
    spread = jnp.mean(centered * centered, axis=-1, keepdims=True)
    return centered * lax.rsqrt(spread + 1e-05) * gain + bias


def widen(rows, weight, bias):
    return (
        jnp.dot(
            lax.all_gather(rows, ("wa", "wb"), axis=0, tiled=True),
            weight,
            preferred_element_type=jnp.float32,
        )
        + bias
    )


def narrow(values, weight):
    return lax.psum_scatter(
        jnp.dot(values, weight, preferred_element_type=jnp.float32).astype(jnp.bfloat16),
        ("wa", "wb"),
        scatter_dimension=0,
        tiled=True,
    ).astype(jnp.float32)


def collective_local(
    tokens,
    deal,
    lengths,
    group_ids,
    page_table,
    prefix_cache,
    qkv_weight,
    qkv_bias,
    out_weight,
    out_bias,
    norm1_gain,
    norm1_bias,
    up_weight,
    up_bias,
    down_weight,
    down_bias,
    norm2_gain,
    norm2_bias,
):
    scale = 1.0 / math.sqrt(HEAD)
    tok_count = lax.axis_size("tok")
    block_devs = lax.axis_size("wa") * lax.axis_size("wb")
    row_dev, width = tokens.shape
    run_len = row_dev // tok_count
    arrived = lax.all_to_all(
        tokens.reshape(tok_count, run_len, width), "tok", split_axis=0, concat_axis=0, tiled=True
    ).reshape(row_dev, width)
    source = deal // (block_devs * row_dev) * run_len + deal % run_len
    ordered = jnp.take(arrived, source, axis=0)
    quarter = qkv_weight.shape[2]
    heads_dev = quarter // HEAD
    qkv = widen(
        ordered, qkv_weight.reshape(width, 3 * quarter), qkv_bias.reshape(3 * quarter)
    ).astype(jnp.bfloat16)
    tok_dev = qkv.shape[0]
    qkv = qkv.reshape(tok_dev, 3, quarter)
    cache_out = qkv[:, 1:3, :]
    queries = qkv[:, 0].reshape(tok_dev, heads_dev, HEAD)
    keys = qkv[:, 1].reshape(tok_dev, heads_dev, HEAD)
    values = qkv[:, 2].reshape(tok_dev, heads_dev, HEAD)
    ends = jnp.cumsum(lengths[0])
    places = jnp.arange(tok_dev, dtype=jnp.int32)
    seq = jnp.sum((places[:, None] >= ends[None, :]).astype(jnp.int32), axis=1)
    seq_ids = jnp.arange(SEQ_DEV, dtype=jnp.int32)
    row_group = jnp.sum(
        jnp.where(seq[:, None] == seq_ids[None, :], group_ids[0][None, :], 0), axis=1
    )
    allowed = (seq[:, None] == seq[None, :]) & (places[None, :] <= places[:, None])
    near = jnp.einsum("qhd,khd->hqk", queries, keys, preferred_element_type=jnp.float32) * scale
    near = jnp.where(allowed[None], near, -jnp.inf)
    best = jnp.max(near, axis=2)
    near_weight = jnp.exp(near - best[:, :, None])
    total = jnp.sum(near_weight, axis=2)
    accum = jnp.einsum(
        "hqk,khd->hqd", near_weight.astype(jnp.bfloat16), values, preferred_element_type=jnp.float32
    )
    pool_size = tok_count * prefix_cache.shape[0]
    page_len = prefix_cache.shape[1]
    slot_ids = jnp.arange(pool_size, dtype=jnp.int32)
    matches = (page_table[:, :, None] == slot_ids[None, None, :]).astype(jnp.int32)
    hits = jnp.sum(matches, axis=1)
    group_range = jnp.arange(page_table.shape[0], dtype=jnp.int32)
    owner_group = jnp.sum(hits * group_range[:, None], axis=0)
    slot_group = jnp.where(jnp.sum(hits, axis=0) > 0, owner_group, -1)
    piece = lax.all_gather(prefix_cache, "tok", axis=0, tiled=True)
    count = piece.shape[0]
    step = math.gcd(count, 8)
    blocks = count // step
    unused_slot = (slot_group < 0).astype(jnp.int32)
    live_first = jnp.argsort(unused_slot, stable=True)
    live_count = count - jnp.sum(unused_slot)
    sorted_groups = jnp.take(slot_group, live_first, axis=0)

    def one_block(carry, index):

        def compute(carry_in):
            top, weight_sum, summed = carry_in
            picks = lax.dynamic_slice_in_dim(live_first, index * step, step, 0)
            pair = jnp.take(piece, picks, axis=0).reshape(step * page_len, 2, heads_dev, HEAD)
            block_groups = lax.dynamic_slice_in_dim(sorted_groups, index * step, step, 0)
            groups = jnp.broadcast_to(block_groups[:, None], (step, page_len)).reshape(
                step * page_len
            )
            far = (
                jnp.einsum("qhd,khd->hqk", queries, pair[:, 0], preferred_element_type=jnp.float32)
                * scale
            )
            far = jnp.where((groups[None, :] == row_group[:, None])[None], far, -jnp.inf)
            new_top = jnp.maximum(top, jnp.max(far, axis=2))
            factor = jnp.exp(top - new_top)
            far_weight = jnp.exp(far - new_top[:, :, None])
            weight_sum = weight_sum * factor + jnp.sum(far_weight, axis=2)
            summed = summed * factor[:, :, None] + jnp.einsum(
                "hqk,khd->hqd",
                far_weight.astype(jnp.bfloat16),
                pair[:, 1],
                preferred_element_type=jnp.float32,
            )
            return (new_top, weight_sum, summed)

        def keep(carry_in):
            return carry_in

        return (lax.cond(index * step < live_count, compute, keep, carry), None)

    result, unused = lax.scan(one_block, (best, total, accum), jnp.arange(blocks, dtype=jnp.int32))
    best, total, accum = result
    attention = (
        (accum / total[:, :, None])
        .transpose(1, 0, 2)
        .reshape(tok_dev, quarter)
        .astype(jnp.bfloat16)
    )
    mixed = narrow(attention, out_weight) + out_bias + ordered.astype(jnp.float32)
    normed = layer_norm(mixed, norm1_gain, norm1_bias).astype(jnp.bfloat16)
    raised = widen(normed, up_weight, up_bias)
    inner = jax.nn.gelu(raised, approximate=False).astype(jnp.bfloat16)
    outer = narrow(inner, down_weight) + down_bias + normed.astype(jnp.float32)
    hidden = layer_norm(outer, norm2_gain, norm2_bias).astype(jnp.bfloat16)
    return (hidden, cache_out)


def layer_kernel(
    n_tok,
    tokens,
    deal,
    lengths,
    group_ids,
    page_table,
    own_kv,
    qkv_w_hbm,
    qkv_b,
    out_w_hbm,
    out_b,
    gain1,
    bias1,
    up_w_hbm,
    up_b,
    down_w_hbm,
    down_b,
    gain2,
    bias2,
    hidden,
    kv_out,
    qkv_w,
    out_w,
    up_w,
    down_w,
    arrived,
    x_all,
    kv_all,
    far_k,
    far_v,
    queries,
    attended,
    part_send,
    part_recv,
    wide_send,
    wide_recv,
    n_all,
    kept,
    w_sem,
    deal_s,
    deal_r,
    kv_s,
    kv_r,
    x_s,
    x_r,
    p_s,
    p_r,
    n_s,
    n_r,
):
    tok = lax.axis_index("tok")
    a = lax.axis_index("wa")
    b = lax.axis_index("wb")
    rows, width = tokens.shape
    run = rows // n_tok
    quarter = qkv_b.shape[1] // 3
    heads = quarter // HEAD
    groups, pages = page_table.shape
    page_len = own_kv.shape[2]
    far_len = pages * page_len
    depth = n_tok // 2
    z, y = tok // 2, tok % 2
    own = a * 2 + b
    near_core = a * 2 + (1 - b)
    across = (1 - a) * 2 + b
    corner = (1 - a) * 2 + (1 - b)
    core_peer = (tok, a, 1 - b)
    x_peer = (tok, 1 - a, b)

    loads = [
        pltpu.make_async_copy(src, dst, w_sem.at[i])
        for i, (src, dst) in enumerate(
            ((qkv_w_hbm, qkv_w), (out_w_hbm, out_w), (up_w_hbm, up_w), (down_w_hbm, down_w))
        )
    ]
    for load in loads:
        load.start()

    barrier = pltpu.get_barrier_semaphore()
    for d in range(1, n_tok):
        pl.semaphore_signal(
            barrier, inc=1, device_id=(lax.rem(tok + d, n_tok), a, b), device_id_type=MESH
        )
    for peer in (core_peer, x_peer):
        pl.semaphore_signal(barrier, inc=1, device_id=peer, device_id_type=MESH)
    pl.semaphore_wait(barrier, n_tok + 1)

    def remote(src, dst, send_sem, recv_sem, peer):
        return pltpu.make_async_remote_copy(
            src_ref=src,
            dst_ref=dst,
            send_sem=send_sem,
            recv_sem=recv_sem,
            device_id=peer,
            device_id_type=MESH,
        )

    def run_at(index):
        return pl.ds(pl.multiple_of(index * run, run), run)

    deals = []
    for d in range(1, n_tok):
        to = lax.rem(tok + d, n_tok)
        copy = remote(
            tokens.at[run_at(to)], arrived.at[run_at(tok)], deal_s.at[d], deal_r.at[d], (to, a, b)
        )
        copy.start()
        deals.append(copy)

    RIGHT, LEFT, PAIR = 0, 1, 2

    def kv_peer(way):
        if way == PAIR:
            return (z * 2 + (1 - y), a, b)
        step = 1 if way == RIGHT else -1
        return ((z + step) * 2 + y, a, b)

    def kv_copy(source, slot, way, from_own):
        held = kv_all.at[source, slot]
        return remote(
            own_kv.at[slot] if from_own else held,
            held,
            kv_s.at[source, slot, way],
            kv_r.at[source, slot],
            kv_peer(way),
        )

    def kv_each(source, slot, ways, action, from_own=False):
        for way in ways:
            if way == PAIR:
                action(kv_copy(source, slot, way, from_own))
            else:

                @pl.when((z < depth - 1) if way == RIGHT else (z > 0))
                def _():
                    action(kv_copy(source, slot, way, from_own))

    def begin(copy):
        copy.start()

    def sent(copy):
        copy.wait_send()

    def kv_arrived(source, slot):
        kv_copy(source, slot, PAIR, False).wait_recv()

    other = z * 2 + (1 - y)
    kv_each(tok, 1, (PAIR,), begin, True)
    kv_each(tok, 0, (RIGHT, LEFT), begin, True)
    kv_each(tok, 1, (RIGHT, LEFT), begin, True)
    kv_each(tok, 0, (PAIR,), begin, True)
    kv_all[tok] = own_kv[...]

    def kv_step(distance):
        if distance == 0:
            kv_arrived(other, 1)
            kv_each(other, 1, (RIGHT, LEFT), begin)
            return
        for way, base in ((RIGHT, z - distance), (LEFT, z + distance)):

            @pl.when((base >= 0) & (base < depth))
            def _():
                same, cross = base * 2 + y, base * 2 + (1 - y)
                kv_arrived(same, 0)
                kv_each(same, 0, (way, PAIR), begin)
                kv_arrived(same, 1)
                kv_each(same, 1, (way,), begin)
                kv_arrived(cross, 1)
                kv_each(cross, 1, (way,), begin)

    def kv_finish():
        for base in range(depth):
            kv_arrived(base * 2 + (1 - y), 0)
        kv_each(tok, 0, (RIGHT, LEFT, PAIR), sent, True)
        kv_each(tok, 1, (RIGHT, LEFT, PAIR), sent, True)
        kv_each(other, 1, (RIGHT, LEFT), sent)
        for distance in range(1, depth):
            for way, base in ((RIGHT, z - distance), (LEFT, z + distance)):

                @pl.when((base >= 0) & (base < depth))
                def _():
                    same, cross = base * 2 + y, base * 2 + (1 - y)
                    kv_each(same, 0, (way, PAIR), sent)
                    kv_each(same, 1, (way,), sent)
                    kv_each(cross, 1, (way,), sent)

    arrived[run_at(tok)] = tokens[run_at(tok)]
    places = deal[...]
    source = places // (4 * rows) * run + lax.rem(places, run)
    hot = jnp.where(
        lax.broadcasted_iota(jnp.int32, (rows, rows), 0) == jnp.broadcast_to(source, (rows, rows)),
        1.0,
        0.0,
    )
    pick = hot.T.astype(jnp.bfloat16)
    for copy in deals:
        copy.wait_recv()
    x_all[own] = jnp.dot(pick, arrived[...], preferred_element_type=jnp.float32).astype(
        jnp.bfloat16
    )

    half = rows // 2

    def spread(buffer, send_sems, recv_sems):
        outs = []
        for part in range(2):
            piece = pl.ds(part * half, half)
            outs.append(
                remote(
                    buffer.at[own, piece],
                    buffer.at[own, piece],
                    send_sems.at[0, part],
                    recv_sems.at[0, part],
                    x_peer,
                )
            )
            outs[-1].start()
        outs.append(
            remote(buffer.at[own], buffer.at[own], send_sems.at[1, 0], recv_sems.at[1, 0], core_peer)
        )
        outs[-1].start()
        return outs

    def pass_on(buffer, send_sems, recv_sems, outs):
        for part in range(2):
            piece = pl.ds(part * half, half)
            outs[part].wait_recv()
            outs.append(
                remote(
                    buffer.at[across, piece],
                    buffer.at[across, piece],
                    send_sems.at[2, part],
                    recv_sems.at[2, part],
                    core_peer,
                )
            )
            outs[-1].start()

    def rows_of(block):
        return pl.ds(pl.multiple_of(block * rows, rows), rows)

    def project(block):
        result = jnp.dot(x_all[block], qkv_w[...], preferred_element_type=jnp.float32) + qkv_b[...]
        result = result.astype(jnp.bfloat16)
        where = rows_of(block)
        queries[where] = result[:, :quarter] * jnp.bfloat16(1.0 / math.sqrt(HEAD))
        kv_out[0, where] = result[:, quarter : 2 * quarter]
        kv_out[1, where] = result[:, 2 * quarter :]

    x_copies = spread(x_all, x_s, x_r)
    kv_step(0)
    loads[0].wait()
    project(own)
    x_copies[2].wait_recv()
    project(near_core)
    kv_step(1)
    pass_on(x_all, x_s, x_r, x_copies)
    project(across)
    for copy in x_copies[3:5]:
        copy.wait_recv()
    project(corner)
    for distance in range(2, depth):
        kv_step(distance)
    kv_finish()
    for load in loads[1:]:
        load.wait()

    for group in range(groups):
        for page in range(pages):
            slot = page_table[group, page]
            spot = pl.ds((group * pages + page) * page_len, page_len)
            far_k[spot] = kv_all[slot // 2, slot % 2, 0]
            far_v[spot] = kv_all[slot // 2, slot % 2, 1]

    near_len = rows * (1 + -(-(MOST_LEN - 1) // rows))
    back = near_len // rows - 1
    contract = (((1,), (1,)), ((), ()))
    lane_head = lax.broadcasted_iota(jnp.int32, (1, quarter), 1) // HEAD

    def attend(block):
        first = jnp.maximum(block - back, 0) * rows
        near = pl.ds(pl.multiple_of(first, rows), near_len)
        query = queries[rows_of(block)]
        place = lax.broadcasted_iota(jnp.int32, (rows, 1), 0) + block * rows
        low = jnp.zeros((rows, 1), jnp.int32)
        group = jnp.zeros((rows, 1), jnp.int32) + group_ids[0, 0]
        end = lengths[0, 0]
        for e in range(1, SEQ_DEV):
            low = jnp.where(place >= end, end, low)
            group = jnp.where(place >= end, group_ids[0, e], group)
            end = end + lengths[0, e]
        key_place = lax.broadcasted_iota(jnp.int32, (rows, near_len), 1) + first
        allowed = (key_place >= low) & (key_place <= place)

        def one_head(head, carry):
            lanes = lane_head == head
            mine = jnp.where(lanes, query, jnp.bfloat16(0))
            score = lax.dot_general(
                mine, kv_out[0, near], contract, preferred_element_type=jnp.float32
            )
            score = jnp.where(allowed, score, -jnp.inf)
            top = jnp.max(score, axis=1, keepdims=True)
            fars = []
            for g in range(groups):
                far = lax.dot_general(
                    mine,
                    far_k[pl.ds(g * far_len, far_len)],
                    contract,
                    preferred_element_type=jnp.float32,
                )
                fars.append(far)
                best = jnp.max(far, axis=1, keepdims=True)
                top = jnp.where(group == g, jnp.maximum(top, best), top)
            weight = jnp.exp(score - top)
            total = jnp.sum(weight, axis=1, keepdims=True)
            summed = jnp.dot(
                weight.astype(jnp.bfloat16), kv_out[1, near], preferred_element_type=jnp.float32
            )
            for g in range(groups):
                weight = jnp.exp(fars[g] - jnp.where(group == g, top, FAR))
                total = total + jnp.sum(weight, axis=1, keepdims=True)
                summed = summed + jnp.dot(
                    weight.astype(jnp.bfloat16),
                    far_v[pl.ds(g * far_len, far_len)],
                    preferred_element_type=jnp.float32,
                )
            attended[...] = jnp.where(lanes, summed / total, attended[...])
            return carry

        attended[...] = jnp.zeros_like(attended)
        lax.fori_loop(0, heads, one_head, 0)
        return jnp.dot(
            attended[...].astype(jnp.bfloat16), out_w[...], preferred_element_type=jnp.float32
        )

    def to_core(phase, index, value):
        part_send[phase, index] = value.astype(jnp.bfloat16)
        copy = remote(
            part_send.at[phase, index],
            part_recv.at[phase, index],
            p_s.at[phase, index],
            p_r.at[phase, index],
            core_peer,
        )
        copy.start()
        return copy

    def to_across(phase, value):
        wide_send[phase] = value.astype(jnp.bfloat16)
        copy = remote(
            wide_send.at[phase], wide_recv.at[phase], p_s.at[phase, 2], p_r.at[phase, 2], x_peer
        )
        copy.start()
        return copy

    def norm(values, gain, bias):
        mean = jnp.mean(values, axis=1, keepdims=True)
        centered = values - mean
        spread_of = jnp.mean(centered * centered, axis=1, keepdims=True)
        return centered * lax.rsqrt(spread_of + 1e-05) * gain[...] + bias[...]

    sums = [to_core(0, 0, attend(corner))]
    value = attend(across)
    sums[0].wait_recv()
    sums.append(to_across(0, value + part_recv[0, 0].astype(jnp.float32)))
    sums.append(to_core(0, 1, attend(near_core)))
    value = attend(own) + out_b[...] + x_all[own].astype(jnp.float32)
    sums[2].wait_recv()
    value = value + part_recv[0, 1].astype(jnp.float32)
    sums[1].wait_recv()
    value = value + wide_recv[0].astype(jnp.float32)
    n_all[own] = norm(value, gain1, bias1).astype(jnp.bfloat16)

    def feed(block):
        raised = (
            jnp.dot(n_all[block], up_w[...], preferred_element_type=jnp.float32) + up_b[...]
        )
        inner = raised * (1.0 + lax.erf(raised * (1.0 / math.sqrt(2.0)))) * 0.5
        return jnp.dot(
            inner.astype(jnp.bfloat16), down_w[...], preferred_element_type=jnp.float32
        )

    n_copies = spread(n_all, n_s, n_r)
    kept[0] = feed(own) + down_b[...] + n_all[own].astype(jnp.float32)
    n_copies[2].wait_recv()
    sums.append(to_core(1, 1, feed(near_core)))
    pass_on(n_all, n_s, n_r, n_copies)
    kept[1] = feed(across)
    for copy in n_copies[3:5]:
        copy.wait_recv()
    sums.append(to_core(1, 0, feed(corner)))
    sums[4].wait_recv()
    sums.append(to_across(1, kept[1] + part_recv[1, 0].astype(jnp.float32)))
    sums[3].wait_recv()
    value = kept[0] + part_recv[1, 1].astype(jnp.float32)
    sums[5].wait_recv()
    value = value + wide_recv[1].astype(jnp.float32)
    hidden[...] = norm(value, gain2, bias2).astype(jnp.bfloat16)
    for copy in deals + x_copies + n_copies + sums:
        copy.wait_send()


def kernel_local(
    tokens,
    deal,
    lengths,
    group_ids,
    page_table,
    prefix_cache,
    qkv_weight,
    qkv_bias,
    out_weight,
    out_bias,
    norm1_gain,
    norm1_bias,
    up_weight,
    up_bias,
    down_weight,
    down_bias,
    norm2_gain,
    norm2_bias,
):
    n_tok = lax.axis_size("tok")
    rows, width = tokens.shape
    quarter = qkv_weight.shape[2]
    hidden_dev = up_weight.shape[1]
    slots, page_len = prefix_cache.shape[:2]
    groups, pages = page_table.shape
    far_keys = groups * pages * page_len
    block_rows = 4 * rows
    vmem = pl.BlockSpec(memory_space=pltpu.VMEM)
    smem = pl.BlockSpec(memory_space=pltpu.SMEM)
    anywhere = pl.BlockSpec(memory_space=pl.ANY)
    dma = pltpu.SemaphoreType.DMA
    half = jnp.bfloat16
    hidden, kv_out = pl.pallas_call(
        functools.partial(layer_kernel, n_tok),
        out_shape=(
            jax.ShapeDtypeStruct((rows, width), half),
            jax.ShapeDtypeStruct((2, block_rows, quarter), half),
        ),
        in_specs=[
            vmem, vmem, smem, smem, smem, vmem, anywhere, vmem, anywhere,
            vmem, vmem, vmem, anywhere, vmem, anywhere, vmem, vmem, vmem,
        ],
        out_specs=(vmem, vmem),
        scratch_shapes=[
            pltpu.VMEM((width, 3 * quarter), half),
            pltpu.VMEM((quarter, width), half),
            pltpu.VMEM((width, hidden_dev), half),
            pltpu.VMEM((hidden_dev, width), half),
            pltpu.VMEM((rows, width), half),
            pltpu.VMEM((4, rows, width), half),
            pltpu.VMEM((n_tok, slots, 2, page_len, quarter), half),
            pltpu.VMEM((far_keys, quarter), half),
            pltpu.VMEM((far_keys, quarter), half),
            pltpu.VMEM((block_rows, quarter), half),
            pltpu.VMEM((rows, quarter), jnp.float32),
            pltpu.VMEM((2, 2, rows, width), half),
            pltpu.VMEM((2, 2, rows, width), half),
            pltpu.VMEM((2, rows, width), half),
            pltpu.VMEM((2, rows, width), half),
            pltpu.VMEM((4, rows, width), half),
            pltpu.VMEM((2, rows, width), jnp.float32),
            dma((4,)),
            dma((n_tok,)),
            dma((n_tok,)),
            dma((n_tok, slots, 3)),
            dma((n_tok, slots)),
            dma((3, 2)),
            dma((3, 2)),
            dma((2, 3)),
            dma((2, 3)),
            dma((3, 2)),
            dma((3, 2)),
        ],
        compiler_params=pltpu.CompilerParams(
            collective_id=0, has_side_effects=True, vmem_limit_bytes=56 * 2**20
        ),
    )(
        tokens,
        deal.reshape(1, rows),
        lengths,
        group_ids,
        page_table,
        prefix_cache.transpose(0, 2, 1, 3),
        qkv_weight.reshape(width, 3 * quarter),
        qkv_bias.reshape(1, 3 * quarter),
        out_weight,
        out_bias.reshape(1, width),
        norm1_gain.reshape(1, width),
        norm1_bias.reshape(1, width),
        up_weight,
        up_bias.reshape(1, hidden_dev),
        down_weight,
        down_bias.reshape(1, width),
        norm2_gain.reshape(1, width),
        norm2_bias.reshape(1, width),
    )
    return (hidden, kv_out.transpose(1, 0, 2))


def solution(mesh):
    tok_count = mesh.shape["tok"]
    fits = tok_count <= 8 and mesh.shape["wa"] == 2 and mesh.shape["wb"] == 2
    return jax.shard_map(
        kernel_local if fits else collective_local,
        mesh=mesh,
        in_specs=(
            P(("tok", "wa", "wb"), None),
            P(("tok", "wa", "wb")),
            P("tok", None),
            P("tok", None),
            P(),
            P("tok", None, None, ("wa", "wb")),
            P(None, None, ("wa", "wb")),
            P(None, ("wa", "wb")),
            P(("wa", "wb"), None),
            P(),
            P(),
            P(),
            P(None, ("wa", "wb")),
            P(("wa", "wb")),
            P(("wa", "wb"), None),
            P(),
            P(),
            P(),
        ),
        out_specs=(P(("tok", "wa", "wb"), None), P("tok", None, ("wa", "wb"))),
        check_vma=False,
    )
```

```python
import functools
import math

import jax
import jax.numpy as jnp
from jax import lax
from jax.experimental import pallas as pl
from jax.experimental.pallas import tpu as pltpu
from jax.sharding import PartitionSpec as P

HEAD = 64
SEQ_DEV = 8
MOST_LEN = 192
PARTS = 2
FAR = 3e38
MESH = pl.DeviceIdType.MESH


def layer_norm(values, gain, bias):
    mean = jnp.mean(values, axis=-1, keepdims=True)
    centered = values - mean
    spread = jnp.mean(centered * centered, axis=-1, keepdims=True)
    return centered * lax.rsqrt(spread + 1e-05) * gain + bias


def widen(rows, weight, bias):
    return (
        jnp.dot(
            lax.all_gather(rows, ("wa", "wb"), axis=0, tiled=True),
            weight,
            preferred_element_type=jnp.float32,
        )
        + bias
    )


def narrow(values, weight):
    return lax.psum_scatter(
        jnp.dot(values, weight, preferred_element_type=jnp.float32).astype(jnp.bfloat16),
        ("wa", "wb"),
        scatter_dimension=0,
        tiled=True,
    ).astype(jnp.float32)


def collective_local(
    tokens,
    deal,
    lengths,
    group_ids,
    page_table,
    prefix_cache,
    qkv_weight,
    qkv_bias,
    out_weight,
    out_bias,
    norm1_gain,
    norm1_bias,
    up_weight,
    up_bias,
    down_weight,
    down_bias,
    norm2_gain,
    norm2_bias,
):
    scale = 1.0 / math.sqrt(HEAD)
    tok_count = lax.axis_size("tok")
    block_devs = lax.axis_size("wa") * lax.axis_size("wb")
    row_dev, width = tokens.shape
    run_len = row_dev // tok_count
    arrived = lax.all_to_all(
        tokens.reshape(tok_count, run_len, width), "tok", split_axis=0, concat_axis=0, tiled=True
    ).reshape(row_dev, width)
    source = deal // (block_devs * row_dev) * run_len + deal % run_len
    ordered = jnp.take(arrived, source, axis=0)
    quarter = qkv_weight.shape[2]
    heads_dev = quarter // HEAD
    qkv = widen(
        ordered, qkv_weight.reshape(width, 3 * quarter), qkv_bias.reshape(3 * quarter)
    ).astype(jnp.bfloat16)
    tok_dev = qkv.shape[0]
    qkv = qkv.reshape(tok_dev, 3, quarter)
    cache_out = qkv[:, 1:3, :]
    queries = qkv[:, 0].reshape(tok_dev, heads_dev, HEAD)
    keys = qkv[:, 1].reshape(tok_dev, heads_dev, HEAD)
    values = qkv[:, 2].reshape(tok_dev, heads_dev, HEAD)
    ends = jnp.cumsum(lengths[0])
    places = jnp.arange(tok_dev, dtype=jnp.int32)
    seq = jnp.sum((places[:, None] >= ends[None, :]).astype(jnp.int32), axis=1)
    seq_ids = jnp.arange(SEQ_DEV, dtype=jnp.int32)
    row_group = jnp.sum(
        jnp.where(seq[:, None] == seq_ids[None, :], group_ids[0][None, :], 0), axis=1
    )
    allowed = (seq[:, None] == seq[None, :]) & (places[None, :] <= places[:, None])
    near = jnp.einsum("qhd,khd->hqk", queries, keys, preferred_element_type=jnp.float32) * scale
    near = jnp.where(allowed[None], near, -jnp.inf)
    best = jnp.max(near, axis=2)
    near_weight = jnp.exp(near - best[:, :, None])
    total = jnp.sum(near_weight, axis=2)
    accum = jnp.einsum(
        "hqk,khd->hqd", near_weight.astype(jnp.bfloat16), values, preferred_element_type=jnp.float32
    )
    pool_size = tok_count * prefix_cache.shape[0]
    page_len = prefix_cache.shape[1]
    slot_ids = jnp.arange(pool_size, dtype=jnp.int32)
    matches = (page_table[:, :, None] == slot_ids[None, None, :]).astype(jnp.int32)
    hits = jnp.sum(matches, axis=1)
    group_range = jnp.arange(page_table.shape[0], dtype=jnp.int32)
    owner_group = jnp.sum(hits * group_range[:, None], axis=0)
    slot_group = jnp.where(jnp.sum(hits, axis=0) > 0, owner_group, -1)
    piece = lax.all_gather(prefix_cache, "tok", axis=0, tiled=True)
    count = piece.shape[0]
    step = math.gcd(count, 8)
    blocks = count // step
    unused_slot = (slot_group < 0).astype(jnp.int32)
    live_first = jnp.argsort(unused_slot, stable=True)
    live_count = count - jnp.sum(unused_slot)
    sorted_groups = jnp.take(slot_group, live_first, axis=0)

    def one_block(carry, index):

        def compute(carry_in):
            top, weight_sum, summed = carry_in
            picks = lax.dynamic_slice_in_dim(live_first, index * step, step, 0)
            pair = jnp.take(piece, picks, axis=0).reshape(step * page_len, 2, heads_dev, HEAD)
            block_groups = lax.dynamic_slice_in_dim(sorted_groups, index * step, step, 0)
            groups = jnp.broadcast_to(block_groups[:, None], (step, page_len)).reshape(
                step * page_len
            )
            far = (
                jnp.einsum("qhd,khd->hqk", queries, pair[:, 0], preferred_element_type=jnp.float32)
                * scale
            )
            far = jnp.where((groups[None, :] == row_group[:, None])[None], far, -jnp.inf)
            new_top = jnp.maximum(top, jnp.max(far, axis=2))
            factor = jnp.exp(top - new_top)
            far_weight = jnp.exp(far - new_top[:, :, None])
            weight_sum = weight_sum * factor + jnp.sum(far_weight, axis=2)
            summed = summed * factor[:, :, None] + jnp.einsum(
                "hqk,khd->hqd",
                far_weight.astype(jnp.bfloat16),
                pair[:, 1],
                preferred_element_type=jnp.float32,
            )
            return (new_top, weight_sum, summed)

        def keep(carry_in):
            return carry_in

        return (lax.cond(index * step < live_count, compute, keep, carry), None)

    result, unused = lax.scan(one_block, (best, total, accum), jnp.arange(blocks, dtype=jnp.int32))
    best, total, accum = result
    attention = (
        (accum / total[:, :, None])
        .transpose(1, 0, 2)
        .reshape(tok_dev, quarter)
        .astype(jnp.bfloat16)
    )
    mixed = narrow(attention, out_weight) + out_bias + ordered.astype(jnp.float32)
    normed = layer_norm(mixed, norm1_gain, norm1_bias).astype(jnp.bfloat16)
    raised = widen(normed, up_weight, up_bias)
    inner = jax.nn.gelu(raised, approximate=False).astype(jnp.bfloat16)
    outer = narrow(inner, down_weight) + down_bias + normed.astype(jnp.float32)
    hidden = layer_norm(outer, norm2_gain, norm2_bias).astype(jnp.bfloat16)
    return (hidden, cache_out)


def layer_kernel(
    n_tok,
    tokens,
    deal,
    lengths,
    group_ids,
    page_table,
    own_kv,
    qkv_w_hbm,
    qkv_b,
    out_w_hbm,
    out_b,
    gain1,
    bias1,
    up_w_hbm,
    up_b,
    down_w_hbm,
    down_b,
    gain2,
    bias2,
    hidden,
    kv_out_hbm,
    qkv_w,
    out_w,
    up_w,
    down_w,
    arrived,
    x_all,
    kv_all,
    kv_out,
    far_k,
    far_v,
    queries,
    attended,
    part_send,
    part_recv,
    wide_send,
    wide_recv,
    n_all,
    kept,
    w_sem,
    deal_s,
    deal_r,
    kv_s,
    kv_r,
    x_s,
    x_r,
    p_s,
    p_r,
    n_s,
    n_r,
):
    tok = lax.axis_index("tok")
    a = lax.axis_index("wa")
    b = lax.axis_index("wb")
    rows, width = tokens.shape
    run = rows // n_tok
    quarter = qkv_b.shape[1]
    heads = quarter // HEAD
    groups, pages = page_table.shape
    page_len = own_kv.shape[2]
    far_len = pages * page_len
    depth = n_tok // 2
    z, y = tok // 2, tok % 2
    own = a * 2 + b
    near_core = a * 2 + (1 - b)
    across = (1 - a) * 2 + b
    corner = (1 - a) * 2 + (1 - b)
    core_peer = (tok, a, 1 - b)
    x_peer = (tok, 1 - a, b)

    def run_at(index):
        return pl.ds(pl.multiple_of(index * run, run), run)

    pairs = (
        (tokens.at[run_at(tok)], arrived.at[run_at(tok)]),
        (qkv_w_hbm, qkv_w),
        (out_w_hbm, out_w),
        (up_w_hbm, up_w),
        (down_w_hbm, down_w),
        (own_kv, kv_all.at[tok]),
    )
    loads = [
        pltpu.make_async_copy(src, dst, w_sem.at[i])
        for i, (src, dst) in enumerate(pairs)
    ]
    barrier = pltpu.get_barrier_semaphore()
    for d in range(1, n_tok):
        pl.semaphore_signal(
            barrier, inc=1, device_id=(lax.rem(tok + d, n_tok), a, b), device_id_type=MESH
        )
    for peer in (core_peer, x_peer):
        pl.semaphore_signal(barrier, inc=1, device_id=peer, device_id_type=MESH)
    for load in loads[:1]:
        load.start()
    pl.semaphore_wait(barrier, n_tok + 1)

    def remote(src, dst, send_sem, recv_sem, peer):
        return pltpu.make_async_remote_copy(
            src_ref=src,
            dst_ref=dst,
            send_sem=send_sem,
            recv_sem=recv_sem,
            device_id=peer,
            device_id_type=MESH,
        )

    deals = []
    for d in range(1, n_tok):
        to = lax.rem(tok + d, n_tok)
        copy = remote(
            tokens.at[run_at(to)], arrived.at[run_at(tok)], deal_s.at[d], deal_r.at[d], (to, a, b)
        )
        copy.start()
        deals.append(copy)

    RIGHT, LEFT, PAIR = 0, 1, 2

    def kv_peer(way):
        if way == PAIR:
            return (z * 2 + (1 - y), a, b)
        step = 1 if way == RIGHT else -1
        return ((z + step) * 2 + y, a, b)

    def kv_copy(source, slot, way, from_own):
        held = kv_all.at[source, slot]
        return remote(
            own_kv.at[slot] if from_own else held,
            held,
            kv_s.at[source, slot, way],
            kv_r.at[source, slot],
            kv_peer(way),
        )

    def kv_each(source, slot, ways, action, from_own=False):
        for way in ways:
            if way == PAIR:
                action(kv_copy(source, slot, way, from_own))
            else:

                @pl.when((z < depth - 1) if way == RIGHT else (z > 0))
                def _():
                    action(kv_copy(source, slot, way, from_own))

    def begin(copy):
        copy.start()

    def sent(copy):
        copy.wait_send()

    def kv_arrived(source, slot):
        kv_copy(source, slot, PAIR, False).wait_recv()

    for slot in range(2):
        kv_each(tok, slot, (RIGHT, LEFT, PAIR), begin, True)
    for load in loads[1:]:
        load.start()

    def kv_along(distance, action):
        for way, base in ((RIGHT, z - distance), (LEFT, z + distance)):

            @pl.when((base >= 0) & (base < depth))
            def _():
                action(base * 2 + y, way)

    def kv_step(distance, slot):
        def onward(source, way):
            kv_arrived(source, slot)
            kv_each(source, slot, (way, PAIR), begin)

        if distance < depth:
            kv_along(distance, onward)

    def kv_finish():
        for distance in range(depth):

            def wait_pair(source, way):
                for slot in range(2):
                    kv_arrived(source + 1 - 2 * y, slot)

            if distance == 0:
                wait_pair(tok, PAIR)
            else:
                kv_along(distance, wait_pair)

    def kv_drain():
        for slot in range(2):
            kv_each(tok, slot, (RIGHT, LEFT, PAIR), sent, True)
        for distance in range(1, depth):

            def drain(source, way):
                for slot in range(2):
                    kv_each(source, slot, (way, PAIR), sent)

            kv_along(distance, drain)

    places = deal[...]
    source = places // (4 * rows) * run + lax.rem(places, run)
    hot = jnp.where(
        lax.broadcasted_iota(jnp.int32, (rows, rows), 0) == jnp.broadcast_to(source, (rows, rows)),
        1.0,
        0.0,
    )
    pick = hot.T.astype(jnp.bfloat16)
    loads[0].wait()
    for copy in deals:
        copy.wait_recv()
    x_all[own] = jnp.dot(pick, arrived[...], preferred_element_type=jnp.float32).astype(
        jnp.bfloat16
    )

    half = rows // PARTS

    def piece(part):
        return pl.ds(part * half, half)

    def rows_to(buffer, block, part, way, send_sems, recv_sems, peer):
        copy = remote(
            buffer.at[block, piece(part)],
            buffer.at[block, piece(part)],
            send_sems.at[way, part],
            recv_sems.at[way, part],
            peer,
        )
        copy.start()
        return copy

    def rows_of(block):
        return pl.ds(pl.multiple_of(block * rows, rows), rows)

    def project(block):
        where = rows_of(block)
        states = x_all[block]
        for part in range(3):
            result = jnp.dot(states, qkv_w[part], preferred_element_type=jnp.float32)
            result = (result + qkv_b[part : part + 1]).astype(jnp.bfloat16)
            if part == 0:
                queries[where] = result * jnp.bfloat16(1.0 / math.sqrt(HEAD))
            else:
                kv_out[part - 1, where] = result

    x_in = [rows_to(x_all, own, part, 0, x_s, x_r, x_peer) for part in range(PARTS)]
    x_core = [rows_to(x_all, own, part, 1, x_s, x_r, core_peer) for part in range(PARTS)]
    x_pass = []
    kv_step(1, 0)
    loads[1].wait()
    project(own)
    kv_step(1, 1)
    for copy in x_core:
        copy.wait_recv()
    project(near_core)
    for part in range(PARTS):
        x_in[part].wait_recv()
        x_pass.append(rows_to(x_all, across, part, 2, x_s, x_r, core_peer))
        if part == 0:
            kv_step(2, 0)
    project(across)
    kv_step(2, 1)
    for copy in x_pass:
        copy.wait_recv()
    project(corner)
    cache_out = pltpu.make_async_copy(kv_out, kv_out_hbm, w_sem.at[6])
    cache_out.start()
    for distance in range(3, depth):
        for slot in range(2):
            kv_step(distance, slot)
    for load in loads[2:]:
        load.wait()
    kv_finish()

    for group in range(groups):
        for page in range(pages):
            slot = page_table[group, page]
            spot = pl.ds((group * pages + page) * page_len, page_len)
            far_k[spot] = kv_all[slot // 2, slot % 2, 0]
            far_v[spot] = kv_all[slot // 2, slot % 2, 1]

    near_len = rows * (1 + -(-(MOST_LEN - 1) // rows))
    back = near_len // rows - 1
    contract = (((1,), (1,)), ((), ()))
    lane_head = lax.broadcasted_iota(jnp.int32, (1, quarter), 1) // HEAD

    def attend(block):
        first = jnp.maximum(block - back, 0) * rows
        near = pl.ds(pl.multiple_of(first, rows), near_len)
        query = queries[rows_of(block)]
        place = lax.broadcasted_iota(jnp.int32, (rows, 1), 0) + block * rows
        low = jnp.zeros((rows, 1), jnp.int32)
        group = jnp.zeros((rows, 1), jnp.int32) + group_ids[0, 0]
        end = lengths[0, 0]
        for e in range(1, SEQ_DEV):
            low = jnp.where(place >= end, end, low)
            group = jnp.where(place >= end, group_ids[0, e], group)
            end = end + lengths[0, e]
        key_place = lax.broadcasted_iota(jnp.int32, (rows, near_len), 1) + first
        allowed = (key_place >= low) & (key_place <= place)

        def one_head(head, carry):
            lanes = lane_head == head
            mine = jnp.where(lanes, query, jnp.bfloat16(0))
            score = lax.dot_general(
                mine, kv_out[0, near], contract, preferred_element_type=jnp.float32
            )
            score = jnp.where(allowed, score, -jnp.inf)
            top = jnp.max(score, axis=1, keepdims=True)
            fars = []
            for g in range(groups):
                far = lax.dot_general(
                    mine,
                    far_k[pl.ds(g * far_len, far_len)],
                    contract,
                    preferred_element_type=jnp.float32,
                )
                fars.append(far)
                best = jnp.max(far, axis=1, keepdims=True)
                top = jnp.where(group == g, jnp.maximum(top, best), top)
            weight = jnp.exp(score - top)
            total = jnp.sum(weight, axis=1, keepdims=True)
            summed = jnp.dot(
                weight.astype(jnp.bfloat16), kv_out[1, near], preferred_element_type=jnp.float32
            )
            for g in range(groups):
                weight = jnp.exp(fars[g] - jnp.where(group == g, top, FAR))
                total = total + jnp.sum(weight, axis=1, keepdims=True)
                summed = summed + jnp.dot(
                    weight.astype(jnp.bfloat16),
                    far_v[pl.ds(g * far_len, far_len)],
                    preferred_element_type=jnp.float32,
                )
            attended[...] = jnp.where(lanes, summed / total, attended[...])
            return carry

        attended[...] = jnp.zeros_like(attended)
        lax.fori_loop(0, heads, one_head, 0)
        return jnp.dot(
            attended[...].astype(jnp.bfloat16), out_w[...], preferred_element_type=jnp.float32
        )

    def to_core(phase, index, part, value):
        where = (phase, index) if part is None else (phase, index, piece(part))
        sem = (phase, index, part or 0)
        part_send[where] = value.astype(jnp.bfloat16)
        copy = remote(
            part_send.at[where], part_recv.at[where], p_s.at[sem], p_r.at[sem], core_peer
        )
        copy.start()
        return copy

    def to_across(phase, part, value):
        where = (phase, piece(part))
        wide_send[where] = value.astype(jnp.bfloat16)
        copy = remote(
            wide_send.at[where],
            wide_recv.at[where],
            p_s.at[phase, 2, part],
            p_r.at[phase, 2, part],
            x_peer,
        )
        copy.start()
        return copy

    def got(ref, *where):
        return ref[where].astype(jnp.float32)

    def norm(values, gain, bias):
        mean = jnp.mean(values, axis=1, keepdims=True)
        centered = values - mean
        spread_of = jnp.mean(centered * centered, axis=1, keepdims=True)
        return centered * lax.rsqrt(spread_of + 1e-05) * gain[...] + bias[...]

    corner_copy = to_core(0, 0, None, attend(corner))
    kept[1] = attend(across)
    corner_copy.wait_recv()
    wide = [
        to_across(0, part, kept[1, piece(part)] + got(part_recv, 0, 0, piece(part)))
        for part in range(PARTS)
    ]
    core_copy = to_core(0, 1, None, attend(near_core))
    kept[0] = attend(own) + out_b[...] + got(x_all, own)
    core_copy.wait_recv()
    sums = [corner_copy, core_copy] + wide
    n_in, n_core, n_pass = [], [], []
    for part in range(PARTS):
        value = kept[0, piece(part)] + got(part_recv, 0, 1, piece(part))
        wide[part].wait_recv()
        value = value + got(wide_recv, 0, piece(part))
        n_all[own, piece(part)] = norm(value, gain1, bias1).astype(jnp.bfloat16)
        n_in.append(rows_to(n_all, own, part, 0, n_s, n_r, x_peer))
        n_core.append(rows_to(n_all, own, part, 1, n_s, n_r, core_peer))

    def feed(states):
        raised = jnp.dot(states, up_w[...], preferred_element_type=jnp.float32) + up_b[...]
        inner = raised * (1.0 + lax.erf(raised * (1.0 / math.sqrt(2.0)))) * 0.5
        return jnp.dot(
            inner.astype(jnp.bfloat16), down_w[...], preferred_element_type=jnp.float32
        )

    kept[0] = feed(n_all[own]) + down_b[...] + got(n_all, own)
    for copy in n_core:
        copy.wait_recv()
    core_copy = to_core(1, 1, None, feed(n_all[near_core]))
    sums.append(core_copy)
    wide = []
    for part in range(PARTS):
        n_in[part].wait_recv()
        n_pass.append(rows_to(n_all, across, part, 2, n_s, n_r, core_peer))
        kept[1, piece(part)] = feed(n_all[across, piece(part)])
        n_pass[part].wait_recv()
        corner_copy = to_core(1, 0, part, feed(n_all[corner, piece(part)]))
        sums.append(corner_copy)
        corner_copy.wait_recv()
        wide.append(
            to_across(1, part, kept[1, piece(part)] + got(part_recv, 1, 0, piece(part)))
        )
    core_copy.wait_recv()
    for part in range(PARTS):
        value = kept[0, piece(part)] + got(part_recv, 1, 1, piece(part))
        wide[part].wait_recv()
        value = value + got(wide_recv, 1, piece(part))
        hidden[piece(part)] = norm(value, gain2, bias2).astype(jnp.bfloat16)
    for copy in deals + x_in + x_core + x_pass + n_in + n_core + n_pass + sums + wide:
        copy.wait_send()
    kv_drain()
    cache_out.wait()


def kernel_local(
    tokens,
    deal,
    lengths,
    group_ids,
    page_table,
    prefix_cache,
    qkv_weight,
    qkv_bias,
    out_weight,
    out_bias,
    norm1_gain,
    norm1_bias,
    up_weight,
    up_bias,
    down_weight,
    down_bias,
    norm2_gain,
    norm2_bias,
):
    n_tok = lax.axis_size("tok")
    rows, width = tokens.shape
    quarter = qkv_weight.shape[2]
    hidden_dev = up_weight.shape[1]
    slots, page_len = prefix_cache.shape[:2]
    groups, pages = page_table.shape
    far_keys = groups * pages * page_len
    block_rows = 4 * rows
    vmem = pl.BlockSpec(memory_space=pltpu.VMEM)
    smem = pl.BlockSpec(memory_space=pltpu.SMEM)
    anywhere = pl.BlockSpec(memory_space=pl.ANY)
    dma = pltpu.SemaphoreType.DMA
    half = jnp.bfloat16
    hidden, kv_out = pl.pallas_call(
        functools.partial(layer_kernel, n_tok),
        out_shape=(
            jax.ShapeDtypeStruct((rows, width), half),
            jax.ShapeDtypeStruct((2, block_rows, quarter), half),
        ),
        in_specs=[
            anywhere, vmem, smem, smem, smem, anywhere, anywhere, vmem, anywhere,
            vmem, vmem, vmem, anywhere, vmem, anywhere, vmem, vmem, vmem,
        ],
        out_specs=(vmem, anywhere),
        scratch_shapes=[
            pltpu.VMEM((3, width, quarter), half),
            pltpu.VMEM((quarter, width), half),
            pltpu.VMEM((width, hidden_dev), half),
            pltpu.VMEM((hidden_dev, width), half),
            pltpu.VMEM((rows, width), half),
            pltpu.VMEM((4, rows, width), half),
            pltpu.VMEM((n_tok, slots, 2, page_len, quarter), half),
            pltpu.VMEM((2, block_rows, quarter), half),
            pltpu.VMEM((far_keys, quarter), half),
            pltpu.VMEM((far_keys, quarter), half),
            pltpu.VMEM((block_rows, quarter), half),
            pltpu.VMEM((rows, quarter), jnp.float32),
            pltpu.VMEM((2, 2, rows, width), half),
            pltpu.VMEM((2, 2, rows, width), half),
            pltpu.VMEM((2, rows, width), half),
            pltpu.VMEM((2, rows, width), half),
            pltpu.VMEM((4, rows, width), half),
            pltpu.VMEM((2, rows, width), jnp.float32),
            dma((7,)),
            dma((n_tok,)),
            dma((n_tok,)),
            dma((n_tok, slots, 3)),
            dma((n_tok, slots)),
            dma((3, PARTS)),
            dma((3, PARTS)),
            dma((2, 3, PARTS)),
            dma((2, 3, PARTS)),
            dma((3, PARTS)),
            dma((3, PARTS)),
        ],
        compiler_params=pltpu.CompilerParams(
            collective_id=0, has_side_effects=True, vmem_limit_bytes=56 * 2**20
        ),
    )(
        tokens,
        deal.reshape(1, rows),
        lengths,
        group_ids,
        page_table,
        prefix_cache.transpose(0, 2, 1, 3),
        qkv_weight.transpose(1, 0, 2),
        qkv_bias,
        out_weight,
        out_bias.reshape(1, width),
        norm1_gain.reshape(1, width),
        norm1_bias.reshape(1, width),
        up_weight,
        up_bias.reshape(1, hidden_dev),
        down_weight,
        down_bias.reshape(1, width),
        norm2_gain.reshape(1, width),
        norm2_bias.reshape(1, width),
    )
    return (hidden, kv_out.transpose(1, 0, 2))


def solution(mesh):
    tok_count = mesh.shape["tok"]
    fits = tok_count <= 8 and mesh.shape["wa"] == 2 and mesh.shape["wb"] == 2
    return jax.shard_map(
        kernel_local if fits else collective_local,
        mesh=mesh,
        in_specs=(
            P(("tok", "wa", "wb"), None),
            P(("tok", "wa", "wb")),
            P("tok", None),
            P("tok", None),
            P(),
            P("tok", None, None, ("wa", "wb")),
            P(None, None, ("wa", "wb")),
            P(None, ("wa", "wb")),
            P(("wa", "wb"), None),
            P(),
            P(),
            P(),
            P(None, ("wa", "wb")),
            P(("wa", "wb")),
            P(("wa", "wb"), None),
            P(),
            P(),
            P(),
        ),
        out_specs=(P(("tok", "wa", "wb"), None), P("tok", None, ("wa", "wb"))),
        check_vma=False,
    )
```

```python
import functools
import math

import jax
import jax.numpy as jnp
from jax import lax
from jax.experimental import pallas as pl
from jax.experimental.pallas import tpu as pltpu
from jax.sharding import PartitionSpec as P

HEAD = 64
SEQ_DEV = 8
MOST_LEN = 192
PARTS = 2
FAR = 3e38
MESH = pl.DeviceIdType.MESH


def layer_norm(values, gain, bias):
    mean = jnp.mean(values, axis=-1, keepdims=True)
    centered = values - mean
    spread = jnp.mean(centered * centered, axis=-1, keepdims=True)
    return centered * lax.rsqrt(spread + 1e-05) * gain + bias


def widen(rows, weight, bias):
    return (
        jnp.dot(
            lax.all_gather(rows, ("wa", "wb"), axis=0, tiled=True),
            weight,
            preferred_element_type=jnp.float32,
        )
        + bias
    )


def narrow(values, weight):
    return lax.psum_scatter(
        jnp.dot(values, weight, preferred_element_type=jnp.float32).astype(jnp.bfloat16),
        ("wa", "wb"),
        scatter_dimension=0,
        tiled=True,
    ).astype(jnp.float32)


def collective_local(
    tokens,
    deal,
    lengths,
    group_ids,
    page_table,
    prefix_cache,
    qkv_weight,
    qkv_bias,
    out_weight,
    out_bias,
    norm1_gain,
    norm1_bias,
    up_weight,
    up_bias,
    down_weight,
    down_bias,
    norm2_gain,
    norm2_bias,
):
    scale = 1.0 / math.sqrt(HEAD)
    tok_count = lax.axis_size("tok")
    block_devs = lax.axis_size("wa") * lax.axis_size("wb")
    row_dev, width = tokens.shape
    run_len = row_dev // tok_count
    arrived = lax.all_to_all(
        tokens.reshape(tok_count, run_len, width), "tok", split_axis=0, concat_axis=0, tiled=True
    ).reshape(row_dev, width)
    source = deal // (block_devs * row_dev) * run_len + deal % run_len
    ordered = jnp.take(arrived, source, axis=0)
    quarter = qkv_weight.shape[2]
    heads_dev = quarter // HEAD
    qkv = widen(
        ordered, qkv_weight.reshape(width, 3 * quarter), qkv_bias.reshape(3 * quarter)
    ).astype(jnp.bfloat16)
    tok_dev = qkv.shape[0]
    qkv = qkv.reshape(tok_dev, 3, quarter)
    cache_out = qkv[:, 1:3, :]
    queries = qkv[:, 0].reshape(tok_dev, heads_dev, HEAD)
    keys = qkv[:, 1].reshape(tok_dev, heads_dev, HEAD)
    values = qkv[:, 2].reshape(tok_dev, heads_dev, HEAD)
    ends = jnp.cumsum(lengths[0])
    places = jnp.arange(tok_dev, dtype=jnp.int32)
    seq = jnp.sum((places[:, None] >= ends[None, :]).astype(jnp.int32), axis=1)
    seq_ids = jnp.arange(SEQ_DEV, dtype=jnp.int32)
    row_group = jnp.sum(
        jnp.where(seq[:, None] == seq_ids[None, :], group_ids[0][None, :], 0), axis=1
    )
    allowed = (seq[:, None] == seq[None, :]) & (places[None, :] <= places[:, None])
    near = jnp.einsum("qhd,khd->hqk", queries, keys, preferred_element_type=jnp.float32) * scale
    near = jnp.where(allowed[None], near, -jnp.inf)
    best = jnp.max(near, axis=2)
    near_weight = jnp.exp(near - best[:, :, None])
    total = jnp.sum(near_weight, axis=2)
    accum = jnp.einsum(
        "hqk,khd->hqd", near_weight.astype(jnp.bfloat16), values, preferred_element_type=jnp.float32
    )
    pool_size = tok_count * prefix_cache.shape[0]
    page_len = prefix_cache.shape[1]
    slot_ids = jnp.arange(pool_size, dtype=jnp.int32)
    matches = (page_table[:, :, None] == slot_ids[None, None, :]).astype(jnp.int32)
    hits = jnp.sum(matches, axis=1)
    group_range = jnp.arange(page_table.shape[0], dtype=jnp.int32)
    owner_group = jnp.sum(hits * group_range[:, None], axis=0)
    slot_group = jnp.where(jnp.sum(hits, axis=0) > 0, owner_group, -1)
    piece = lax.all_gather(prefix_cache, "tok", axis=0, tiled=True)
    count = piece.shape[0]
    step = math.gcd(count, 8)
    blocks = count // step
    unused_slot = (slot_group < 0).astype(jnp.int32)
    live_first = jnp.argsort(unused_slot, stable=True)
    live_count = count - jnp.sum(unused_slot)
    sorted_groups = jnp.take(slot_group, live_first, axis=0)

    def one_block(carry, index):

        def compute(carry_in):
            top, weight_sum, summed = carry_in
            picks = lax.dynamic_slice_in_dim(live_first, index * step, step, 0)
            pair = jnp.take(piece, picks, axis=0).reshape(step * page_len, 2, heads_dev, HEAD)
            block_groups = lax.dynamic_slice_in_dim(sorted_groups, index * step, step, 0)
            groups = jnp.broadcast_to(block_groups[:, None], (step, page_len)).reshape(
                step * page_len
            )
            far = (
                jnp.einsum("qhd,khd->hqk", queries, pair[:, 0], preferred_element_type=jnp.float32)
                * scale
            )
            far = jnp.where((groups[None, :] == row_group[:, None])[None], far, -jnp.inf)
            new_top = jnp.maximum(top, jnp.max(far, axis=2))
            factor = jnp.exp(top - new_top)
            far_weight = jnp.exp(far - new_top[:, :, None])
            weight_sum = weight_sum * factor + jnp.sum(far_weight, axis=2)
            summed = summed * factor[:, :, None] + jnp.einsum(
                "hqk,khd->hqd",
                far_weight.astype(jnp.bfloat16),
                pair[:, 1],
                preferred_element_type=jnp.float32,
            )
            return (new_top, weight_sum, summed)

        def keep(carry_in):
            return carry_in

        return (lax.cond(index * step < live_count, compute, keep, carry), None)

    result, unused = lax.scan(one_block, (best, total, accum), jnp.arange(blocks, dtype=jnp.int32))
    best, total, accum = result
    attention = (
        (accum / total[:, :, None])
        .transpose(1, 0, 2)
        .reshape(tok_dev, quarter)
        .astype(jnp.bfloat16)
    )
    mixed = narrow(attention, out_weight) + out_bias + ordered.astype(jnp.float32)
    normed = layer_norm(mixed, norm1_gain, norm1_bias).astype(jnp.bfloat16)
    raised = widen(normed, up_weight, up_bias)
    inner = jax.nn.gelu(raised, approximate=False).astype(jnp.bfloat16)
    outer = narrow(inner, down_weight) + down_bias + normed.astype(jnp.float32)
    hidden = layer_norm(outer, norm2_gain, norm2_bias).astype(jnp.bfloat16)
    return (hidden, cache_out)


def layer_kernel(
    n_tok,
    tokens,
    deal,
    lengths,
    group_ids,
    page_table,
    own_kv,
    qkv_w_hbm,
    qkv_b,
    out_w_hbm,
    out_b,
    gain1,
    bias1,
    up_w_hbm,
    up_b,
    down_w_hbm,
    down_b,
    gain2,
    bias2,
    hidden,
    kv_out_hbm,
    qkv_w,
    out_w,
    up_w,
    down_w,
    arrived,
    x_all,
    kv_all,
    kv_out,
    kv_pair,
    far_k,
    far_v,
    queries,
    near_sum,
    near_top,
    near_total,
    far_sum,
    far_top,
    far_total,
    part_send,
    part_recv,
    wide_send,
    wide_recv,
    n_all,
    kept,
    w_sem,
    deal_s,
    deal_r,
    kv_s,
    kv_r,
    x_s,
    x_r,
    p_s,
    p_r,
    n_s,
    n_r,
):
    tok = lax.axis_index("tok")
    a = lax.axis_index("wa")
    b = lax.axis_index("wb")
    rows, width = tokens.shape
    run = rows // n_tok
    quarter = qkv_b.shape[1]
    heads = quarter // HEAD
    groups, pages = page_table.shape
    page_len = own_kv.shape[2]
    far_len = pages * page_len
    depth = n_tok // 2
    z, y = tok // 2, tok % 2
    own = a * 2 + b
    near_core = a * 2 + (1 - b)
    across = (1 - a) * 2 + b
    corner = (1 - a) * 2 + (1 - b)
    core_peer = (tok, a, 1 - b)
    x_peer = (tok, 1 - a, b)

    def run_at(index):
        return pl.ds(pl.multiple_of(index * run, run), run)

    pairs = (
        (tokens.at[run_at(tok)], arrived.at[run_at(tok)]),
        (qkv_w_hbm, qkv_w),
        (out_w_hbm, out_w),
        (up_w_hbm, up_w),
        (down_w_hbm, down_w),
        (own_kv, kv_all.at[tok]),
    )
    loads = [
        pltpu.make_async_copy(src, dst, w_sem.at[i])
        for i, (src, dst) in enumerate(pairs)
    ]
    barrier = pltpu.get_barrier_semaphore()
    for d in range(1, n_tok):
        pl.semaphore_signal(
            barrier, inc=1, device_id=(lax.rem(tok + d, n_tok), a, b), device_id_type=MESH
        )
    for peer in (core_peer, x_peer):
        pl.semaphore_signal(barrier, inc=1, device_id=peer, device_id_type=MESH)
    for load in loads[:1]:
        load.start()
    pl.semaphore_wait(barrier, n_tok + 1)

    def remote(src, dst, send_sem, recv_sem, peer):
        return pltpu.make_async_remote_copy(
            src_ref=src,
            dst_ref=dst,
            send_sem=send_sem,
            recv_sem=recv_sem,
            device_id=peer,
            device_id_type=MESH,
        )

    deals = []
    for d in range(1, n_tok):
        to = lax.rem(tok + d, n_tok)
        copy = remote(
            tokens.at[run_at(to)], arrived.at[run_at(tok)], deal_s.at[d], deal_r.at[d], (to, a, b)
        )
        copy.start()
        deals.append(copy)

    RIGHT, LEFT, PAIR = 0, 1, 2

    def kv_peer(way):
        if way == PAIR:
            return (z * 2 + (1 - y), a, b)
        step = 1 if way == RIGHT else -1
        return ((z + step) * 2 + y, a, b)

    def kv_copy(source, slot, way, from_own):
        held = kv_all.at[source, slot]
        return remote(
            own_kv.at[slot] if from_own else held,
            held,
            kv_s.at[source, slot, way],
            kv_r.at[source, slot],
            kv_peer(way),
        )

    def kv_each(source, slot, ways, action, from_own=False):
        for way in ways:
            if way == PAIR:
                action(kv_copy(source, slot, way, from_own))
            else:

                @pl.when((z < depth - 1) if way == RIGHT else (z > 0))
                def _():
                    action(kv_copy(source, slot, way, from_own))

    def begin(copy):
        copy.start()

    def sent(copy):
        copy.wait_send()

    def kv_arrived(source, slot):
        kv_copy(source, slot, PAIR, False).wait_recv()

    for slot in range(2):
        kv_each(tok, slot, (RIGHT, LEFT, PAIR), begin, True)
    for load in loads[1:]:
        load.start()

    def kv_along(distance, action):
        for way, base in ((RIGHT, z - distance), (LEFT, z + distance)):

            @pl.when((base >= 0) & (base < depth))
            def _():
                action(base * 2 + y, way)

    def kv_step(distance, slot):
        def onward(source, way):
            kv_arrived(source, slot)
            kv_each(source, slot, (way, PAIR), begin)

        if distance < depth:
            kv_along(distance, onward)

    def kv_finish():
        for distance in range(depth):

            def wait_pair(source, way):
                for slot in range(2):
                    kv_arrived(source + 1 - 2 * y, slot)

            if distance == 0:
                wait_pair(tok, PAIR)
            else:
                kv_along(distance, wait_pair)

    def kv_drain():
        for slot in range(2):
            kv_each(tok, slot, (RIGHT, LEFT, PAIR), sent, True)
        for distance in range(1, depth):

            def drain(source, way):
                for slot in range(2):
                    kv_each(source, slot, (way, PAIR), sent)

            kv_along(distance, drain)

    places = deal[...]
    source = places // (4 * rows) * run + lax.rem(places, run)
    hot = jnp.where(
        lax.broadcasted_iota(jnp.int32, (rows, rows), 0) == jnp.broadcast_to(source, (rows, rows)),
        1.0,
        0.0,
    )
    pick = hot.T.astype(jnp.bfloat16)
    loads[0].wait()
    for copy in deals:
        copy.wait_recv()
    x_all[own] = jnp.dot(pick, arrived[...], preferred_element_type=jnp.float32).astype(
        jnp.bfloat16
    )

    half = rows // PARTS

    def piece(part):
        return pl.ds(part * half, half)

    def rows_to(buffer, block, part, way, send_sems, recv_sems, peer):
        copy = remote(
            buffer.at[block, piece(part)],
            buffer.at[block, piece(part)],
            send_sems.at[way, part],
            recv_sems.at[way, part],
            peer,
        )
        copy.start()
        return copy

    def rows_of(block):
        return pl.ds(pl.multiple_of(block * rows, rows), rows)

    def project(block):
        where = rows_of(block)
        states = x_all[block]
        for part in range(3):
            result = jnp.dot(states, qkv_w[part], preferred_element_type=jnp.float32)
            result = (result + qkv_b[part : part + 1]).astype(jnp.bfloat16)
            if part == 0:
                queries[where] = result * jnp.bfloat16(1.0 / math.sqrt(HEAD))
            else:
                kv_out[part - 1, where] = result
        kv_pair[where] = jnp.stack([kv_out[0, where], kv_out[1, where]], axis=1)

    x_in = [rows_to(x_all, own, part, 0, x_s, x_r, x_peer) for part in range(PARTS)]
    x_core = [rows_to(x_all, own, part, 1, x_s, x_r, core_peer) for part in range(PARTS)]
    x_pass = []
    kv_step(1, 0)
    loads[1].wait()
    project(own)
    kv_step(1, 1)
    for copy in x_core:
        copy.wait_recv()
    project(near_core)
    for part in range(PARTS):
        x_in[part].wait_recv()
        x_pass.append(rows_to(x_all, across, part, 2, x_s, x_r, core_peer))
        if part == 0:
            kv_step(2, 0)
    project(across)
    kv_step(2, 1)
    for copy in x_pass:
        copy.wait_recv()
    project(corner)
    cache_out = pltpu.make_async_copy(kv_pair, kv_out_hbm, w_sem.at[6])
    cache_out.start()
    near_len = rows * (1 + -(-(MOST_LEN - 1) // rows))
    back = near_len // rows - 1
    contract = (((1,), (1,)), ((), ()))
    lane_head = lax.broadcasted_iota(jnp.int32, (1, quarter), 1) // HEAD

    def put(ref, where, lanes, value):
        ref[where] = jnp.where(lanes, value, ref[where])

    def attend_near(block):
        first = jnp.maximum(block - back, 0) * rows
        near = pl.ds(pl.multiple_of(first, rows), near_len)
        where = rows_of(block)
        query = queries[where]
        place = lax.broadcasted_iota(jnp.int32, (rows, 1), 0) + block * rows
        low = jnp.zeros((rows, 1), jnp.int32)
        end = lengths[0, 0]
        for e in range(1, SEQ_DEV):
            low = jnp.where(place >= end, end, low)
            end = end + lengths[0, e]
        key_place = lax.broadcasted_iota(jnp.int32, (rows, near_len), 1) + first
        allowed = (key_place >= low) & (key_place <= place)

        def one_head(head, carry):
            lanes = lane_head == head
            mine = jnp.where(lanes, query, jnp.bfloat16(0))
            score = lax.dot_general(
                mine, kv_out[0, near], contract, preferred_element_type=jnp.float32
            )
            score = jnp.where(allowed, score, -jnp.inf)
            top = jnp.max(score, axis=1, keepdims=True)
            weight = jnp.exp(score - top)
            summed = jnp.dot(
                weight.astype(jnp.bfloat16), kv_out[1, near], preferred_element_type=jnp.float32
            )
            put(near_top, where, lanes, top)
            put(near_total, where, lanes, jnp.sum(weight, axis=1, keepdims=True))
            put(near_sum, where, lanes, summed)
            return carry

        lax.fori_loop(0, heads, one_head, 0)

    def attend(block):
        where = rows_of(block)
        query = queries[where]
        place = lax.broadcasted_iota(jnp.int32, (rows, 1), 0) + block * rows
        group = jnp.zeros((rows, 1), jnp.int32) + group_ids[0, 0]
        end = lengths[0, 0]
        for e in range(1, SEQ_DEV):
            group = jnp.where(place >= end, group_ids[0, e], group)
            end = end + lengths[0, e]

        def one_head(head, carry):
            lanes = lane_head == head
            mine = jnp.where(lanes, query, jnp.bfloat16(0))
            fars = []
            top = jnp.full((rows, 1), -jnp.inf, jnp.float32)
            for g in range(groups):
                far = lax.dot_general(
                    mine,
                    far_k[pl.ds(g * far_len, far_len)],
                    contract,
                    preferred_element_type=jnp.float32,
                )
                fars.append(far)
                top = jnp.where(group == g, jnp.max(far, axis=1, keepdims=True), top)
            total = jnp.zeros((rows, 1), jnp.float32)
            summed = jnp.zeros((rows, quarter), jnp.float32)
            for g in range(groups):
                weight = jnp.exp(fars[g] - jnp.where(group == g, top, FAR))
                total = total + jnp.sum(weight, axis=1, keepdims=True)
                summed = summed + jnp.dot(
                    weight.astype(jnp.bfloat16),
                    far_v[pl.ds(g * far_len, far_len)],
                    preferred_element_type=jnp.float32,
                )
            put(far_top, ..., lanes, top)
            put(far_total, ..., lanes, total)
            put(far_sum, ..., lanes, summed)
            return carry

        lax.fori_loop(0, heads, one_head, 0)
        top = jnp.maximum(near_top[where], far_top[...])
        near_share = jnp.exp(near_top[where] - top)
        far_share = jnp.exp(far_top[...] - top)
        total = near_total[where] * near_share + far_total[...] * far_share
        attended = (near_sum[where] * near_share + far_sum[...] * far_share) / total
        return jnp.dot(attended.astype(jnp.bfloat16), out_w[...], preferred_element_type=jnp.float32)

    for ref in (near_sum, near_top, near_total, far_sum, far_top, far_total):
        ref[...] = jnp.zeros_like(ref)
    kv_step(3, 0)
    attend_near(corner)
    attend_near(across)
    kv_step(3, 1)
    attend_near(near_core)
    attend_near(own)
    for distance in range(4, depth):
        for slot in range(2):
            kv_step(distance, slot)
    for load in loads[2:]:
        load.wait()
    kv_finish()

    for group in range(groups):
        for page in range(pages):
            slot = page_table[group, page]
            spot = pl.ds((group * pages + page) * page_len, page_len)
            far_k[spot] = kv_all[slot // 2, slot % 2, 0]
            far_v[spot] = kv_all[slot // 2, slot % 2, 1]

    def to_core(phase, index, part, value):
        where = (phase, index) if part is None else (phase, index, piece(part))
        sem = (phase, index, part or 0)
        part_send[where] = value.astype(jnp.bfloat16)
        copy = remote(
            part_send.at[where], part_recv.at[where], p_s.at[sem], p_r.at[sem], core_peer
        )
        copy.start()
        return copy

    def to_across(phase, part, value):
        where = (phase, piece(part))
        wide_send[where] = value.astype(jnp.bfloat16)
        copy = remote(
            wide_send.at[where],
            wide_recv.at[where],
            p_s.at[phase, 2, part],
            p_r.at[phase, 2, part],
            x_peer,
        )
        copy.start()
        return copy

    def got(ref, *where):
        return ref[where].astype(jnp.float32)

    def norm(values, gain, bias):
        mean = jnp.mean(values, axis=1, keepdims=True)
        centered = values - mean
        spread_of = jnp.mean(centered * centered, axis=1, keepdims=True)
        return centered * lax.rsqrt(spread_of + 1e-05) * gain[...] + bias[...]

    corner_copy = to_core(0, 0, None, attend(corner))
    kept[1] = attend(across)
    corner_copy.wait_recv()
    wide = [
        to_across(0, part, kept[1, piece(part)] + got(part_recv, 0, 0, piece(part)))
        for part in range(PARTS)
    ]
    core_copy = to_core(0, 1, None, attend(near_core))
    kept[0] = attend(own) + out_b[...] + got(x_all, own)
    core_copy.wait_recv()
    sums = [corner_copy, core_copy] + wide
    n_in, n_core, n_pass = [], [], []
    for part in range(PARTS):
        value = kept[0, piece(part)] + got(part_recv, 0, 1, piece(part))
        wide[part].wait_recv()
        value = value + got(wide_recv, 0, piece(part))
        n_all[own, piece(part)] = norm(value, gain1, bias1).astype(jnp.bfloat16)
        n_in.append(rows_to(n_all, own, part, 0, n_s, n_r, x_peer))
        n_core.append(rows_to(n_all, own, part, 1, n_s, n_r, core_peer))

    def feed(states):
        raised = jnp.dot(states, up_w[...], preferred_element_type=jnp.float32) + up_b[...]
        inner = raised * (1.0 + lax.erf(raised * (1.0 / math.sqrt(2.0)))) * 0.5
        return jnp.dot(
            inner.astype(jnp.bfloat16), down_w[...], preferred_element_type=jnp.float32
        )

    kept[0] = feed(n_all[own]) + down_b[...] + got(n_all, own)
    for copy in n_core:
        copy.wait_recv()
    core_copy = to_core(1, 1, None, feed(n_all[near_core]))
    sums.append(core_copy)
    wide = []
    for part in range(PARTS):
        n_in[part].wait_recv()
        n_pass.append(rows_to(n_all, across, part, 2, n_s, n_r, core_peer))
        kept[1, piece(part)] = feed(n_all[across, piece(part)])
        n_pass[part].wait_recv()
        corner_copy = to_core(1, 0, part, feed(n_all[corner, piece(part)]))
        sums.append(corner_copy)
        corner_copy.wait_recv()
        wide.append(
            to_across(1, part, kept[1, piece(part)] + got(part_recv, 1, 0, piece(part)))
        )
    core_copy.wait_recv()
    for part in range(PARTS):
        value = kept[0, piece(part)] + got(part_recv, 1, 1, piece(part))
        wide[part].wait_recv()
        value = value + got(wide_recv, 1, piece(part))
        hidden[piece(part)] = norm(value, gain2, bias2).astype(jnp.bfloat16)
    for copy in deals + x_in + x_core + x_pass + n_in + n_core + n_pass + sums + wide:
        copy.wait_send()
    kv_drain()
    cache_out.wait()


def hand_over(hidden_in, cache_in, hidden_out, cache_out, hidden_held, cache_held, sems):
    into = [
        pltpu.make_async_copy(hidden_in, hidden_held, sems.at[0, 0]),
        pltpu.make_async_copy(cache_in, cache_held, sems.at[1, 0]),
    ]
    out = [
        pltpu.make_async_copy(hidden_held, hidden_out, sems.at[0, 1]),
        pltpu.make_async_copy(cache_held, cache_out, sems.at[1, 1]),
    ]
    for copy in into:
        copy.start()
    for first, then in zip(into, out):
        first.wait()
        then.start()
    for copy in out:
        copy.wait()


def kernel_local(
    tokens,
    deal,
    lengths,
    group_ids,
    page_table,
    prefix_cache,
    qkv_weight,
    qkv_bias,
    out_weight,
    out_bias,
    norm1_gain,
    norm1_bias,
    up_weight,
    up_bias,
    down_weight,
    down_bias,
    norm2_gain,
    norm2_bias,
):
    n_tok = lax.axis_size("tok")
    rows, width = tokens.shape
    quarter = qkv_weight.shape[2]
    hidden_dev = up_weight.shape[1]
    slots, page_len = prefix_cache.shape[:2]
    groups, pages = page_table.shape
    far_keys = groups * pages * page_len
    block_rows = 4 * rows
    vmem = pl.BlockSpec(memory_space=pltpu.VMEM)
    smem = pl.BlockSpec(memory_space=pltpu.SMEM)
    anywhere = pl.BlockSpec(memory_space=pl.ANY)
    dma = pltpu.SemaphoreType.DMA
    half = jnp.bfloat16
    hidden, kv_out = pl.pallas_call(
        functools.partial(layer_kernel, n_tok),
        out_shape=(
            jax.ShapeDtypeStruct((rows, width), half),
            jax.ShapeDtypeStruct((block_rows, 2, quarter), half),
        ),
        in_specs=[
            anywhere, vmem, smem, smem, smem, anywhere, anywhere, vmem, anywhere,
            vmem, vmem, vmem, anywhere, vmem, anywhere, vmem, vmem, vmem,
        ],
        out_specs=(vmem, anywhere),
        scratch_shapes=[
            pltpu.VMEM((3, width, quarter), half),
            pltpu.VMEM((quarter, width), half),
            pltpu.VMEM((width, hidden_dev), half),
            pltpu.VMEM((hidden_dev, width), half),
            pltpu.VMEM((rows, width), half),
            pltpu.VMEM((4, rows, width), half),
            pltpu.VMEM((n_tok, slots, 2, page_len, quarter), half),
            pltpu.VMEM((2, block_rows, quarter), half),
            pltpu.VMEM((block_rows, 2, quarter), half),
            pltpu.VMEM((far_keys, quarter), half),
            pltpu.VMEM((far_keys, quarter), half),
            pltpu.VMEM((block_rows, quarter), half),
            pltpu.VMEM((block_rows, quarter), jnp.float32),
            pltpu.VMEM((block_rows, quarter), jnp.float32),
            pltpu.VMEM((block_rows, quarter), jnp.float32),
            pltpu.VMEM((rows, quarter), jnp.float32),
            pltpu.VMEM((rows, quarter), jnp.float32),
            pltpu.VMEM((rows, quarter), jnp.float32),
            pltpu.VMEM((2, 2, rows, width), half),
            pltpu.VMEM((2, 2, rows, width), half),
            pltpu.VMEM((2, rows, width), half),
            pltpu.VMEM((2, rows, width), half),
            pltpu.VMEM((4, rows, width), half),
            pltpu.VMEM((2, rows, width), jnp.float32),
            dma((7,)),
            dma((n_tok,)),
            dma((n_tok,)),
            dma((n_tok, slots, 3)),
            dma((n_tok, slots)),
            dma((3, PARTS)),
            dma((3, PARTS)),
            dma((2, 3, PARTS)),
            dma((2, 3, PARTS)),
            dma((3, PARTS)),
            dma((3, PARTS)),
        ],
        compiler_params=pltpu.CompilerParams(
            collective_id=0, has_side_effects=True, vmem_limit_bytes=56 * 2**20
        ),
    )(
        tokens,
        deal.reshape(1, rows),
        lengths,
        group_ids,
        page_table,
        prefix_cache.transpose(0, 2, 1, 3),
        qkv_weight.transpose(1, 0, 2),
        qkv_bias,
        out_weight,
        out_bias.reshape(1, width),
        norm1_gain.reshape(1, width),
        norm1_bias.reshape(1, width),
        up_weight,
        up_bias.reshape(1, hidden_dev),
        down_weight,
        down_bias.reshape(1, width),
        norm2_gain.reshape(1, width),
        norm2_bias.reshape(1, width),
    )
    return pl.pallas_call(
        hand_over,
        out_shape=(
            jax.ShapeDtypeStruct(hidden.shape, half),
            jax.ShapeDtypeStruct(kv_out.shape, half),
        ),
        in_specs=[anywhere, anywhere],
        out_specs=(anywhere, anywhere),
        scratch_shapes=[
            pltpu.VMEM(hidden.shape, half),
            pltpu.VMEM(kv_out.shape, half),
            dma((2, 2)),
        ],
    )(hidden, kv_out)


def solution(mesh):
    tok_count = mesh.shape["tok"]
    fits = tok_count <= 8 and mesh.shape["wa"] == 2 and mesh.shape["wb"] == 2
    return jax.shard_map(
        kernel_local if fits else collective_local,
        mesh=mesh,
        in_specs=(
            P(("tok", "wa", "wb"), None),
            P(("tok", "wa", "wb")),
            P("tok", None),
            P("tok", None),
            P(),
            P("tok", None, None, ("wa", "wb")),
            P(None, None, ("wa", "wb")),
            P(None, ("wa", "wb")),
            P(("wa", "wb"), None),
            P(),
            P(),
            P(),
            P(None, ("wa", "wb")),
            P(("wa", "wb")),
            P(("wa", "wb"), None),
            P(),
            P(),
            P(),
        ),
        out_specs=(P(("tok", "wa", "wb"), None), P("tok", None, ("wa", "wb"))),
        check_vma=False,
    )
```
